32 devices in a mesh: pair: 2 (over x), col: 16 (over z, y, core).
Axes of the slice: x: 2, y: 2, z: 4, core: 2. Of those that a mesh axis runs over, the one named last changes fastest.
Arguments:
- amplitudes: bfloat16 [624, 32768], P('pair', 'col'), may hold values from -6 to 6
- integrals: bfloat16 [16, 192, 128, 128], P('col', 'pair'), may hold values from -0.5 to 0.5
- ab_slot: int32 [16, 192], P('col', 'pair'), may hold values from 0 to 15, as said below
- cd_pick: int32 [16, 192], P('col', 'pair'), may hold values from 0 to 31
- wanted: int32 [16, 16, 2], replicated, may hold values from 0 to 15, as said below
- kept_count: int32 [16], replicated, may hold values from 32 to 192, as said below
Outputs:
- residual: bfloat16 [624, 32768], P('pair', 'col')
The draws below stay inside these ranges and needn't reach their ends.
Inputs may be any that keep to these rules, and one draw needn't show every extreme that they name: Within one owner no pair (ab_slot, cd_pick) repeats. `wanted`: for each owner and holder the 2 requested tiles are distinct. `kept_count`: at least one owner has all 192 slots live.
All inputs are finite; a program needn't handle non-finite values.
Results may differ from the reference program's by a relative error of at most 0.001.
Values may be sent and summed in bfloat16 or wider, within the bound.
A program may use at most 128 MiB of HBM per device.

```python
import jax
import jax.numpy as jnp
from jax import lax

TILE = 128
KMAX = 192
ABT_DEV = 16
CDT_DEV = 16
CAP = 2
PAIRS = 624
NCD_T = 256
N_COL = 16


def slot_lists(key):
    keys = jax.random.split(jax.random.fold_in(key, 11), N_COL)
    npick = N_COL * CAP

    def one_owner(owner_key):
        order = jax.random.permutation(jax.random.fold_in(owner_key, 1), npick)
        base = jax.random.randint(jax.random.fold_in(owner_key, 2), (npick,), 0, ABT_DEV)
        index = jnp.arange(KMAX)
        picks = order[index % npick]
        slots = (base[picks] + index // npick) % ABT_DEV
        return jnp.stack([slots, picks]).astype(jnp.int32)
    return jax.vmap(one_owner)(keys).astype(jnp.int32)


def draw_ab_slot(key, part):
    return slot_lists(key)[:, 0, :].astype(jnp.int32)


def draw_cd_pick(key, part):
    return slot_lists(key)[:, 1, :].astype(jnp.int32)


def draw_wanted(key, part):
    keys = jax.random.split(jax.random.fold_in(key, 21), N_COL * N_COL)

    def one_row(row_key):
        return jax.random.permutation(row_key, CDT_DEV)[:CAP]
    return jax.vmap(one_row)(keys).reshape(N_COL, N_COL, CAP).astype(jnp.int32)


def draw_kept_count(key, part):
    divisors = 1 + jax.random.randint(jax.random.fold_in(key, 5), (N_COL,), 0, 6)
    counts = KMAX // divisors
    chosen = jax.random.randint(jax.random.fold_in(key, 6), (), 0, N_COL)
    return jnp.where(jnp.arange(N_COL) == chosen, KMAX, counts).astype(jnp.int32)


def steps_of(own_key, shape, shards, least, top_value):
    loudness, own = 1.0, jax.random.fold_in(own_key, 6)
    for axis_at, shards_of in shards:
        steps = jnp.exp(jax.random.uniform(jax.random.fold_in(own, axis_at), (shards_of,), jnp.float32, least / len(shards), top_value / len(shards)))
        loudness = loudness * jnp.repeat(steps, shape[axis_at] // shards_of).reshape([-1 if axis == axis_at else 1 for axis in range(len(shape))])
    return loudness


def scatter_about(rng, dims, spread, limit, pieces=(), held_as=jnp.bfloat16):
    entries = jax.random.normal(rng, dims, jnp.float32) * spread
    if len(pieces) > 0:
        entries = steps_of(rng, dims, pieces, -0.22, 0.18) * entries
    return jnp.clip(entries, min=-limit, max=limit).astype(held_as)


def setup_inputs(seed: int = 0) -> dict:
    key_list = jax.random.split(jax.random.key(seed), 7)
    return {
        "amplitudes": scatter_about(key_list[0], (PAIRS, NCD_T * TILE), 1.0, 6.0, ((0, 2), (1, 16))),
        "integrals": scatter_about(key_list[1], (N_COL, KMAX, TILE, TILE), TILE ** -0.5, 0.5, ((0, 16), (1, 2))),
        "ab_slot": draw_ab_slot(jax.random.fold_in(key_list[6], 71), 0),
        "cd_pick": draw_cd_pick(jax.random.fold_in(key_list[6], 71), 0),
        "wanted": draw_wanted(jax.random.fold_in(key_list[6], 71), 0),
        "kept_count": draw_kept_count(jax.random.fold_in(key_list[6], 71), 0),
    }


def reference(amplitudes, integrals, ab_slot, cd_pick, wanted, kept_count):
    pairs = amplitudes.shape[0]
    blocks = amplitudes.reshape(pairs, NCD_T, TILE)

    def column(args):
        tiles, ab_list, pick_list, want, count = args
        source = (pick_list // CAP).astype(jnp.int32)
        within = (pick_list % CAP).astype(jnp.int32)
        tile_index = (source * CDT_DEV + want[source, within]).astype(jnp.int32)
        chosen = jnp.take(blocks, tile_index, axis=1).astype(jnp.float32)
        prods = jnp.einsum("pkd,ked->pke", chosen, tiles.astype(jnp.float32), precision=lax.Precision.HIGHEST)
        live = jnp.arange(KMAX) < count
        table = ((ab_list[:, None] == jnp.arange(ABT_DEV)[None, :]) & live[:, None]).astype(jnp.float32)
        return jnp.einsum("pke,ka->pae", prods, table, precision=lax.Precision.HIGHEST)

    outs = lax.map(column, (integrals, ab_slot, cd_pick, wanted, kept_count))
    joined = jnp.transpose(outs, (1, 0, 2, 3)).reshape(pairs, N_COL * ABT_DEV * TILE)
    return joined.astype(jnp.bfloat16)
```

```python
import functools

import jax
import jax.numpy as jnp
from jax import lax
from jax.experimental import pallas as pl
from jax.experimental.pallas import tpu as pltpu
from jax.sharding import PartitionSpec as P

TILE = 128
ABT_DEV = 16
CAP = 2
CHUNKS = 4
MESH = pl.DeviceIdType.MESH


def kernel(
    n_pair, n_col, slots,
    amp_ref, int_ref, ab_ref, pick_ref, wanted_ref, count_ref,
    out_ref,
    tiles, pack, lhs, parts, table_v, table_s, wide,
    tile_sem, own_sem, table_sem, t_send, t_recv, v_send, v_recv, a_send, a_recv, *vall,
):
    pair = lax.axis_index("pair")
    col = lax.axis_index("col")
    n_tiles = n_col * CAP
    depth = CAP * TILE
    places = ABT_DEV * n_tiles
    piece = TILE // CHUNKS
    group = 2 * CHUNKS
    lot_size = 32

    barrier = pltpu.get_barrier_semaphore()

    root = n_col - 1
    last = col == root

    def greet_pair(step, carry):
        peer = lax.rem(pair + step, n_pair)
        pl.semaphore_signal(barrier, inc=1, device_id=(peer, col), device_id_type=MESH)
        return carry

    lax.fori_loop(1, n_pair, greet_pair, 0)

    def v_copy(step, chunk, source):
        peer = lax.rem(pair + step, n_pair)
        return pltpu.make_async_remote_copy(
            src_ref=int_ref.at[0, :, pl.ds(chunk * piece, piece), :],
            dst_ref=vall[chunk].at[pl.ds(source * slots, slots)],
            send_sem=v_send.at[step, chunk],
            recv_sem=v_recv.at[step, chunk],
            device_id=(peer, col),
            device_id_type=MESH,
        )

    def tile_copy(tile):
        return pltpu.make_async_copy(
            amp_ref.at[:, pl.ds(pl.multiple_of(tile * TILE, TILE), TILE)], tiles.at[tile], tile_sem.at[tile]
        )

    n_held = tiles.shape[0]
    for tile in range(n_held):
        tile_copy(tile).start()

    @pl.when(jnp.logical_not(last))
    def _():
        pl.semaphore_wait(barrier, n_pair - 1)
        pl.semaphore_signal(barrier, inc=1, device_id=(pair, root), device_id_type=MESH)

    @pl.when(last)
    def _():
        pl.semaphore_wait(barrier, n_pair - 1 + n_col - 1)

        def release(peer, carry):
            pl.semaphore_signal(barrier, inc=1, device_id=(pair, peer), device_id_type=MESH)
            return carry

        lax.fori_loop(0, n_col - 1, release, 0)

    for chunk in range(CHUNKS):
        for step in range(1, n_pair):
            v_copy(step, chunk, pair).start()

    def own_copy(chunk):
        return pltpu.make_async_copy(
            int_ref.at[0, :, pl.ds(chunk * piece, piece), :],
            vall[chunk].at[pl.ds(pair * slots, slots)],
            own_sem.at[chunk],
        )

    for chunk in range(CHUNKS):
        own_copy(chunk).start()

    lane = lax.broadcasted_iota(jnp.int32, (slots, slots), 1)
    row = lax.broadcasted_iota(jnp.int32, (slots, slots), 0)
    key_row = ab_ref[...] * n_tiles + pick_ref[...]
    key = jnp.sum(jnp.where(lane == row, key_row, 0), axis=1, keepdims=True)
    number = pair * slots + lax.broadcasted_iota(jnp.int32, (slots, 1), 0)
    key = jnp.where(number < count_ref[col], key, -1)
    place = lax.broadcasted_iota(jnp.int32, (slots, places), 1)
    parts[pair] = jnp.sum(jnp.where(place == key, number + 1, 0), axis=0, keepdims=True)
    for chunk in range(CHUNKS):
        vall[chunk][n_pair * slots] = jnp.zeros((piece, TILE), jnp.bfloat16)

    def t_copy(step, source):
        peer = lax.rem(pair + step, n_pair)
        return pltpu.make_async_remote_copy(
            src_ref=parts.at[source],
            dst_ref=parts.at[source],
            send_sem=t_send.at[step],
            recv_sem=t_recv.at[step],
            device_id=(peer, col),
            device_id_type=MESH,
        )

    def a_copy(step, source):
        peer = lax.rem(col + step, n_col)
        return pltpu.make_async_remote_copy(
            src_ref=pack.at[step],
            dst_ref=lhs.at[:, pl.ds(pl.multiple_of(source * depth, depth), depth)],
            send_sem=a_send.at[step],
            recv_sem=a_recv.at[step],
            device_id=(pair, peer),
            device_id_type=MESH,
        )

    for step in range(1, n_pair):
        t_copy(step, pair).start()

    def requested(owner, k):
        return tiles[wanted_ref[owner, k, col]]

    for tile in range(n_held):
        tile_copy(tile).wait()

    @pl.when(jnp.logical_not(last))
    def _():
        pl.semaphore_wait(barrier, 1)

    def send(step, carry):
        owner = lax.rem(col + step, n_col)
        for k in range(CAP):
            pack[step, :, k * TILE : (k + 1) * TILE] = requested(owner, k)
        a_copy(step, col).start()
        return carry

    lax.fori_loop(1, n_col, send, 0)
    for k in range(CAP):
        lhs[:, pl.ds(pl.multiple_of(col * depth + k * TILE, TILE), TILE)] = requested(col, k)

    for step in range(1, n_pair):
        t_copy(step, lax.rem(pair + n_pair - step, n_pair)).wait_recv()
    found = parts[0]
    for index in range(1, n_pair):
        found = found + parts[index]
    table_v[...] = jnp.where(found == 0, n_pair * slots, found - 1)
    to_scalar = pltpu.make_async_copy(table_v, table_s, table_sem)
    to_scalar.start()
    to_scalar.wait()
    for chunk in range(CHUNKS):
        own_copy(chunk).wait()

    def arrived(step, carry):
        a_copy(step, lax.rem(col + n_col - step, n_col)).wait_recv()
        return carry

    lax.fori_loop(1, n_col, arrived, 0)
    n_wide = wide.shape[0]
    for chunk in range(CHUNKS):
        for step in range(1, n_pair):
            v_copy(step, chunk, lax.rem(pair + n_pair - step, n_pair)).wait_recv()
        for block in range(ABT_DEV // group):
            part = block % n_wide
            for inner in range(group):
                first = (block * group + inner) * n_tiles

                def gather(lot, carry):
                    for more in range(lot_size):
                        tile = lot * lot_size + more
                        at = pl.multiple_of(tile * TILE, TILE)
                        wide[part, inner * piece : (inner + 1) * piece, pl.ds(at, TILE)] = vall[chunk][table_s[0, first + tile]]
                    return carry

                lax.fori_loop(0, n_tiles // lot_size, gather, 0)
            total = lax.dot_general(
                lhs[...], wide[part], (((1,), (1,)), ((), ())), preferred_element_type=jnp.float32
            ).astype(jnp.bfloat16)
            for inner in range(group):
                first = (block * group + inner) * TILE + chunk * piece
                out_ref[:, first : first + piece] = total[:, inner * piece : (inner + 1) * piece]

    def sent(step, carry):
        a_copy(step, col).wait_send()
        return carry

    lax.fori_loop(1, n_col, sent, 0)
    for step in range(1, n_pair):
        t_copy(step, pair).wait_send()
        for chunk in range(CHUNKS):
            v_copy(step, chunk, pair).wait_send()


def body(n_pair, n_col, amplitudes, integrals, ab_slot, cd_pick, wanted, kept_count):
    pairs = amplitudes.shape[0]
    slots = integrals.shape[1]
    n_held = amplitudes.shape[1] // TILE
    depth = CAP * TILE
    places = ABT_DEV * n_col * CAP
    n_wide = 2 if n_col <= 16 else 1
    vmem = pl.BlockSpec(memory_space=pltpu.VMEM)
    anywhere = pl.BlockSpec(memory_space=pl.ANY)
    smem = pl.BlockSpec(memory_space=pltpu.SMEM)
    dma = pltpu.SemaphoreType.DMA
    return pl.pallas_call(
        functools.partial(kernel, n_pair, n_col, slots),
        out_shape=jax.ShapeDtypeStruct((pairs, ABT_DEV * TILE), jnp.bfloat16),
        in_specs=[anywhere, anywhere, vmem, vmem, smem, smem],
        out_specs=vmem,
        scratch_shapes=[
            pltpu.VMEM((n_held, pairs, TILE), jnp.bfloat16),
            pltpu.VMEM((n_col, pairs, depth), jnp.bfloat16),
            pltpu.VMEM((pairs, n_col * depth), jnp.bfloat16),
            pltpu.VMEM((n_pair, 1, places), jnp.int32),
            pltpu.VMEM((1, places), jnp.int32),
            pltpu.SMEM((1, places), jnp.int32),
            pltpu.VMEM((n_wide, 2 * TILE, n_col * depth), jnp.bfloat16),
            dma((n_held,)), dma((CHUNKS,)), dma,
            dma((n_pair,)), dma((n_pair,)),
            dma((n_pair, CHUNKS)), dma((n_pair, CHUNKS)),
            dma((n_col,)), dma((n_col,)),
        ]
        + [pltpu.VMEM((n_pair * slots + 1, TILE // CHUNKS, TILE), jnp.bfloat16)] * CHUNKS,
        compiler_params=pltpu.CompilerParams(
            collective_id=0, has_side_effects=True, vmem_limit_bytes=60 * 1024 * 1024
        ),
    )(amplitudes, integrals, ab_slot, cd_pick, jnp.transpose(wanted, (0, 2, 1)), kept_count)


def solution(mesh):
    in_specs = (
        P("pair", "col"),
        P("col", "pair", None, None),
        P("col", "pair"),
        P("col", "pair"),
        P(),
        P(),
    )
    out_specs = P("pair", "col")
    run = functools.partial(body, mesh.shape["pair"], mesh.shape["col"])
    return jax.shard_map(run, mesh=mesh, in_specs=in_specs, out_specs=out_specs, check_vma=False)
```

```python
import functools

import jax
import jax.numpy as jnp
from jax import lax
from jax.experimental import pallas as pl
from jax.experimental.pallas import tpu as pltpu
from jax.sharding import PartitionSpec as P

TILE = 128
ABT_DEV = 16
CAP = 2
CHUNKS = 4
MESH = pl.DeviceIdType.MESH


def kernel(
    n_pair, n_col, slots,
    amp_ref, int_ref, ab_ref, pick_ref, wanted_ref, count_ref,
    out_ref,
    tiles, pack, lhs, parts, table_v, table_s, wide, total_v,
    tile_sem, own_sem, table_sem, t_send, t_recv, v_send, v_recv, a_send, a_recv, *vall,
):
    pair = lax.axis_index("pair")
    col = lax.axis_index("col")
    n_tiles = n_col * CAP
    depth = CAP * TILE
    places = ABT_DEV * n_tiles
    piece = TILE // CHUNKS
    group = 2 * CHUNKS
    lot_size = wide.shape[2] // TILE
    n_lots = n_tiles // lot_size

    barrier = pltpu.get_barrier_semaphore()

    root = n_col - 1
    last = col == root

    def greet_pair(step, carry):
        peer = lax.rem(pair + step, n_pair)
        pl.semaphore_signal(barrier, inc=1, device_id=(peer, col), device_id_type=MESH)
        return carry

    lax.fori_loop(1, n_pair, greet_pair, 0)

    def v_copy(step, chunk, source):
        peer = lax.rem(pair + step, n_pair)
        return pltpu.make_async_remote_copy(
            src_ref=int_ref.at[0, :, pl.ds(chunk * piece, piece), :],
            dst_ref=vall[chunk].at[pl.ds(source * slots, slots)],
            send_sem=v_send.at[step, chunk],
            recv_sem=v_recv.at[step, chunk],
            device_id=(peer, col),
            device_id_type=MESH,
        )

    def tile_copy(tile):
        return pltpu.make_async_copy(
            amp_ref.at[:, pl.ds(pl.multiple_of(tile * TILE, TILE), TILE)], tiles.at[tile], tile_sem.at[tile]
        )

    n_held = tiles.shape[0]
    for tile in range(n_held):
        tile_copy(tile).start()

    def own_copy(chunk):
        return pltpu.make_async_copy(
            int_ref.at[0, :, pl.ds(chunk * piece, piece), :],
            vall[chunk].at[pl.ds(pair * slots, slots)],
            own_sem.at[chunk],
        )

    for chunk in range(CHUNKS):
        own_copy(chunk).start()

    @pl.when(jnp.logical_not(last))
    def _():
        pl.semaphore_wait(barrier, n_pair - 1)
        pl.semaphore_signal(barrier, inc=1, device_id=(pair, root), device_id_type=MESH)

    @pl.when(last)
    def _():
        pl.semaphore_wait(barrier, n_pair - 1 + n_col - 1)

        def release(peer, carry):
            pl.semaphore_signal(barrier, inc=1, device_id=(pair, peer), device_id_type=MESH)
            return carry

        lax.fori_loop(0, n_col - 1, release, 0)

    for step in range(1, n_pair):
        v_copy(step, 0, pair).start()

    lane = lax.broadcasted_iota(jnp.int32, (slots, slots), 1)
    row = lax.broadcasted_iota(jnp.int32, (slots, slots), 0)
    key_row = ab_ref[...] * n_tiles + pick_ref[...]
    key = jnp.sum(jnp.where(lane == row, key_row, 0), axis=1, keepdims=True)
    number = pair * slots + lax.broadcasted_iota(jnp.int32, (slots, 1), 0)
    key = jnp.where(number < count_ref[col], key, -1)
    place = lax.broadcasted_iota(jnp.int32, (slots, places), 1)
    parts[pair] = jnp.sum(jnp.where(place == key, number + 1, 0), axis=0, keepdims=True)
    for chunk in range(CHUNKS):
        vall[chunk][n_pair * slots] = jnp.zeros((piece, TILE), jnp.bfloat16)

    def t_copy(step, source):
        peer = lax.rem(pair + step, n_pair)
        return pltpu.make_async_remote_copy(
            src_ref=parts.at[source],
            dst_ref=parts.at[source],
            send_sem=t_send.at[step],
            recv_sem=t_recv.at[step],
            device_id=(peer, col),
            device_id_type=MESH,
        )

    def a_copy(step, source):
        peer = lax.rem(col + step, n_col)
        return pltpu.make_async_remote_copy(
            src_ref=pack.at[step],
            dst_ref=lhs.at[:, pl.ds(pl.multiple_of(source * depth, depth), depth)],
            send_sem=a_send.at[step],
            recv_sem=a_recv.at[step],
            device_id=(pair, peer),
            device_id_type=MESH,
        )

    for step in range(1, n_pair):
        t_copy(step, pair).start()
    for chunk in range(1, CHUNKS):
        for step in range(1, n_pair):
            v_copy(step, chunk, pair).start()

    def requested(owner, k):
        return tiles[wanted_ref[owner, k, col]]

    for tile in range(n_held):
        tile_copy(tile).wait()

    @pl.when(jnp.logical_not(last))
    def _():
        pl.semaphore_wait(barrier, 1)

    def send(step, carry):
        owner = lax.rem(col + step, n_col)
        for k in range(CAP):
            pack[step, :, k * TILE : (k + 1) * TILE] = requested(owner, k)
        a_copy(step, col).start()
        return carry

    lax.fori_loop(1, n_col, send, 0)
    for k in range(CAP):
        lhs[:, pl.ds(pl.multiple_of(col * depth + k * TILE, TILE), TILE)] = requested(col, k)

    for step in range(1, n_pair):
        t_copy(step, lax.rem(pair + n_pair - step, n_pair)).wait_recv()
    found = parts[0]
    for index in range(1, n_pair):
        found = found + parts[index]
    table_v[...] = jnp.where(found == 0, n_pair * slots, found - 1)
    to_scalar = pltpu.make_async_copy(table_v, table_s, table_sem)
    to_scalar.start()
    to_scalar.wait()
    for chunk in range(CHUNKS):
        own_copy(chunk).wait()

    def arrived(step, carry):
        a_copy(step, lax.rem(col + n_col - step, n_col)).wait_recv()
        return carry

    lax.fori_loop(1, n_col, arrived, 0)
    for chunk in range(CHUNKS):
        for step in range(1, n_pair):
            v_copy(step, chunk, lax.rem(pair + n_pair - step, n_pair)).wait_recv()
        for block in range(ABT_DEV // group):
            part = block % 2

            def lot_dot(lot):
                for inner in range(group):
                    first = (block * group + inner) * n_tiles + lot * lot_size
                    for tile in range(lot_size):
                        wide[part, inner * piece : (inner + 1) * piece, tile * TILE : (tile + 1) * TILE] = vall[chunk][
                            table_s[0, first + tile]
                        ]
                columns = lhs[...] if n_lots == 1 else lhs[:, pl.ds(pl.multiple_of(lot * wide.shape[2], TILE), wide.shape[2])]
                return lax.dot_general(columns, wide[part], (((1,), (1,)), ((), ())), preferred_element_type=jnp.float32)

            def add_lot(lot, carry):
                total_v[...] += lot_dot(lot)
                return carry

            if n_lots == 1:
                total = lot_dot(0)
            else:
                total_v[...] = jnp.zeros_like(total_v)
                lax.fori_loop(0, n_lots, add_lot, 0)
                total = total_v[...]
            total = total.astype(jnp.bfloat16)
            for inner in range(group):
                first = (block * group + inner) * TILE + chunk * piece
                out_ref[:, first : first + piece] = total[:, inner * piece : (inner + 1) * piece]

    def sent(step, carry):
        a_copy(step, col).wait_send()
        return carry

    lax.fori_loop(1, n_col, sent, 0)
    for step in range(1, n_pair):
        t_copy(step, pair).wait_send()
        for chunk in range(CHUNKS):
            v_copy(step, chunk, pair).wait_send()


def body(n_pair, n_col, amplitudes, integrals, ab_slot, cd_pick, wanted, kept_count):
    pairs = amplitudes.shape[0]
    slots = integrals.shape[1]
    n_held = amplitudes.shape[1] // TILE
    depth = CAP * TILE
    places = ABT_DEV * n_col * CAP
    lot_depth = min(16, n_col) * depth
    vmem = pl.BlockSpec(memory_space=pltpu.VMEM)
    anywhere = pl.BlockSpec(memory_space=pl.ANY)
    smem = pl.BlockSpec(memory_space=pltpu.SMEM)
    dma = pltpu.SemaphoreType.DMA
    return pl.pallas_call(
        functools.partial(kernel, n_pair, n_col, slots),
        out_shape=jax.ShapeDtypeStruct((pairs, ABT_DEV * TILE), jnp.bfloat16),
        in_specs=[anywhere, anywhere, vmem, vmem, smem, smem],
        out_specs=vmem,
        scratch_shapes=[
            pltpu.VMEM((n_held, pairs, TILE), jnp.bfloat16),
            pltpu.VMEM((n_col, pairs, depth), jnp.bfloat16),
            pltpu.VMEM((pairs, n_col * depth), jnp.bfloat16),
            pltpu.VMEM((n_pair, 1, places), jnp.int32),
            pltpu.VMEM((1, places), jnp.int32),
            pltpu.SMEM((1, places), jnp.int32),
            pltpu.VMEM((2, 2 * TILE, lot_depth), jnp.bfloat16),
            pltpu.VMEM((pairs, 2 * TILE), jnp.float32),
            dma((n_held,)), dma((CHUNKS,)), dma,
            dma((n_pair,)), dma((n_pair,)),
            dma((n_pair, CHUNKS)), dma((n_pair, CHUNKS)),
            dma((n_col,)), dma((n_col,)),
        ]
        + [pltpu.VMEM((n_pair * slots + 1, TILE // CHUNKS, TILE), jnp.bfloat16)] * CHUNKS,
        compiler_params=pltpu.CompilerParams(
            collective_id=0, has_side_effects=True, vmem_limit_bytes=60 * 1024 * 1024
        ),
    )(amplitudes, integrals, ab_slot, cd_pick, jnp.transpose(wanted, (0, 2, 1)), kept_count)


def solution(mesh):
    in_specs = (
        P("pair", "col"),
        P("col", "pair", None, None),
        P("col", "pair"),
        P("col", "pair"),
        P(),
        P(),
    )
    out_specs = P("pair", "col")
    run = functools.partial(body, mesh.shape["pair"], mesh.shape["col"])
    return jax.shard_map(run, mesh=mesh, in_specs=in_specs, out_specs=out_specs, check_vma=False)
```

```python
import functools

import jax
import jax.numpy as jnp
from jax import lax
from jax.experimental import pallas as pl
from jax.experimental.pallas import tpu as pltpu
from jax.sharding import PartitionSpec as P

TILE = 128
ABT_DEV = 16
CAP = 2
CHUNKS = 4
MESH = pl.DeviceIdType.MESH


def kernel(
    n_pair, n_col, slots,
    amp_ref, int_ref, ab_ref, pick_ref, wanted_ref, count_ref,
    out_ref,
    tiles, pack, lhs, parts, table_v, table_s, wide, total_v,
    tile_sem, own_sem, table_sem, t_send, t_recv, v_send, v_recv, a_send, a_recv, *vall,
):
    pair = lax.axis_index("pair")
    col = lax.axis_index("col")
    n_tiles = n_col * CAP
    depth = CAP * TILE
    places = ABT_DEV * n_tiles
    piece = TILE // CHUNKS
    group = 2 * CHUNKS
    lot_size = wide.shape[2] // TILE
    n_lots = n_tiles // lot_size

    barrier = pltpu.get_barrier_semaphore()

    root = n_col - 1
    last = col == root

    def greet_pair(step, carry):
        peer = lax.rem(pair + step, n_pair)
        pl.semaphore_signal(barrier, inc=1, device_id=(peer, col), device_id_type=MESH)
        return carry

    lax.fori_loop(1, n_pair, greet_pair, 0)

    def v_copy(step, chunk, source):
        peer = lax.rem(pair + step, n_pair)
        return pltpu.make_async_remote_copy(
            src_ref=int_ref.at[0, :, pl.ds(chunk * piece, piece), :],
            dst_ref=vall[chunk].at[pl.ds(source * slots, slots)],
            send_sem=v_send.at[step, chunk],
            recv_sem=v_recv.at[step, chunk],
            device_id=(peer, col),
            device_id_type=MESH,
        )

    def tile_copy(tile):
        return pltpu.make_async_copy(
            amp_ref.at[:, pl.ds(pl.multiple_of(tile * TILE, TILE), TILE)], tiles.at[tile], tile_sem.at[tile]
        )

    n_held = tiles.shape[0]
    for tile in range(n_held):
        tile_copy(tile).start()

    def own_copy(chunk):
        return pltpu.make_async_copy(
            int_ref.at[0, :, pl.ds(chunk * piece, piece), :],
            vall[chunk].at[pl.ds(pair * slots, slots)],
            own_sem.at[chunk],
        )

    for chunk in range(CHUNKS):
        own_copy(chunk).start()

    @pl.when(jnp.logical_not(last))
    def _():
        pl.semaphore_wait(barrier, n_pair - 1)
        pl.semaphore_signal(barrier, inc=1, device_id=(pair, root), device_id_type=MESH)

    @pl.when(last)
    def _():
        pl.semaphore_wait(barrier, n_pair - 1 + n_col - 1)

        def release(peer, carry):
            pl.semaphore_signal(barrier, inc=1, device_id=(pair, peer), device_id_type=MESH)
            return carry

        lax.fori_loop(0, n_col - 1, release, 0)

    for step in range(1, n_pair):
        v_copy(step, 0, pair).start()

    lane = lax.broadcasted_iota(jnp.int32, (slots, slots), 1)
    row = lax.broadcasted_iota(jnp.int32, (slots, slots), 0)
    key_row = ab_ref[...] * n_tiles + pick_ref[...]
    key = jnp.sum(jnp.where(lane == row, key_row, 0), axis=1, keepdims=True)
    number = pair * slots + lax.broadcasted_iota(jnp.int32, (slots, 1), 0)
    key = jnp.where(number < count_ref[col], key, -1)
    place = lax.broadcasted_iota(jnp.int32, (slots, places), 1)
    parts[pair] = jnp.sum(jnp.where(place == key, number + 1, 0), axis=0, keepdims=True)
    for chunk in range(CHUNKS):
        vall[chunk][n_pair * slots] = jnp.zeros((piece, TILE), jnp.bfloat16)

    def t_copy(step, source):
        peer = lax.rem(pair + step, n_pair)
        return pltpu.make_async_remote_copy(
            src_ref=parts.at[source],
            dst_ref=parts.at[source],
            send_sem=t_send.at[step],
            recv_sem=t_recv.at[step],
            device_id=(peer, col),
            device_id_type=MESH,
        )

    def a_copy(step, source):
        peer = lax.rem(col + step, n_col)
        return pltpu.make_async_remote_copy(
            src_ref=pack.at[step],
            dst_ref=lhs.at[:, pl.ds(pl.multiple_of(source * depth, depth), depth)],
            send_sem=a_send.at[step],
            recv_sem=a_recv.at[step],
            device_id=(pair, peer),
            device_id_type=MESH,
        )

    for step in range(1, n_pair):
        t_copy(step, pair).start()
    for chunk in range(1, CHUNKS):
        for step in range(1, n_pair):
            v_copy(step, chunk, pair).start()

    def requested(owner, k):
        return tiles[wanted_ref[owner, k, col]]

    for tile in range(n_held):
        tile_copy(tile).wait()

    @pl.when(jnp.logical_not(last))
    def _():
        pl.semaphore_wait(barrier, 1)

    def send(step, carry):
        owner = lax.rem(col + step, n_col)
        for k in range(CAP):
            pack[step, :, k * TILE : (k + 1) * TILE] = requested(owner, k)
        a_copy(step, col).start()
        return carry

    lax.fori_loop(1, n_col, send, 0)
    for k in range(CAP):
        lhs[:, pl.ds(pl.multiple_of(col * depth + k * TILE, TILE), TILE)] = requested(col, k)

    for step in range(1, n_pair):
        t_copy(step, lax.rem(pair + n_pair - step, n_pair)).wait_recv()
    found = parts[0]
    for index in range(1, n_pair):
        found = found + parts[index]
    table_v[...] = jnp.where(found == 0, n_pair * slots, found - 1)
    to_scalar = pltpu.make_async_copy(table_v, table_s, table_sem)
    to_scalar.start()
    to_scalar.wait()
    for chunk in range(CHUNKS):
        own_copy(chunk).wait()

    def arrived(step, carry):
        a_copy(step, lax.rem(col + n_col - step, n_col)).wait_recv()
        return carry

    lax.fori_loop(1, n_col, arrived, 0)
    for chunk in range(CHUNKS):
        for step in range(1, n_pair):
            v_copy(step, chunk, lax.rem(pair + n_pair - step, n_pair)).wait_recv()
        for block in range(ABT_DEV // group):
            part = block % 2

            def lot_dot(lot):
                for inner in range(group):
                    first = (block * group + inner) * n_tiles + lot * lot_size
                    for tile in range(lot_size):
                        wide[part, inner * piece : (inner + 1) * piece, tile * TILE : (tile + 1) * TILE] = vall[chunk][
                            table_s[0, first + tile]
                        ]
                columns = lhs[...] if n_lots == 1 else lhs[:, pl.ds(pl.multiple_of(lot * wide.shape[2], TILE), wide.shape[2])]
                return lax.dot_general(columns, wide[part], (((1,), (1,)), ((), ())), preferred_element_type=jnp.float32)

            def add_lot(lot, carry):
                total_v[...] += lot_dot(lot)
                return carry

            if n_lots == 1:
                total = lot_dot(0)
            else:
                total_v[...] = jnp.zeros_like(total_v)
                lax.fori_loop(0, n_lots, add_lot, 0)
                total = total_v[...]
            total = total.astype(jnp.bfloat16)
            for inner in range(group):
                first = (block * group + inner) * TILE + chunk * piece
                out_ref[:, first : first + piece] = total[:, inner * piece : (inner + 1) * piece]

    def sent(step, carry):
        a_copy(step, col).wait_send()
        return carry

    lax.fori_loop(1, n_col, sent, 0)
    for step in range(1, n_pair):
        t_copy(step, pair).wait_send()
        for chunk in range(CHUNKS):
            v_copy(step, chunk, pair).wait_send()


def body(n_pair, n_col, amplitudes, integrals, ab_slot, cd_pick, wanted, kept_count):
    pairs = amplitudes.shape[0]
    slots = integrals.shape[1]
    n_held = amplitudes.shape[1] // TILE
    depth = CAP * TILE
    places = ABT_DEV * n_col * CAP
    lot_depth = min(16, n_col) * depth
    vmem = pl.BlockSpec(memory_space=pltpu.VMEM)
    anywhere = pl.BlockSpec(memory_space=pl.ANY)
    smem = pl.BlockSpec(memory_space=pltpu.SMEM)
    dma = pltpu.SemaphoreType.DMA
    return pl.pallas_call(
        functools.partial(kernel, n_pair, n_col, slots),
        out_shape=pltpu.VMEM((pairs, ABT_DEV * TILE), jnp.bfloat16),
        in_specs=[anywhere, anywhere, vmem, vmem, smem, smem],
        out_specs=vmem,
        scratch_shapes=[
            pltpu.VMEM((n_held, pairs, TILE), jnp.bfloat16),
            pltpu.VMEM((n_col, pairs, depth), jnp.bfloat16),
            pltpu.VMEM((pairs, n_col * depth), jnp.bfloat16),
            pltpu.VMEM((n_pair, 1, places), jnp.int32),
            pltpu.VMEM((1, places), jnp.int32),
            pltpu.SMEM((1, places), jnp.int32),
            pltpu.VMEM((2, 2 * TILE, lot_depth), jnp.bfloat16),
            pltpu.VMEM((pairs, 2 * TILE), jnp.float32),
            dma((n_held,)), dma((CHUNKS,)), dma,
            dma((n_pair,)), dma((n_pair,)),
            dma((n_pair, CHUNKS)), dma((n_pair, CHUNKS)),
            dma((n_col,)), dma((n_col,)),
        ]
        + [pltpu.VMEM((n_pair * slots + 1, TILE // CHUNKS, TILE), jnp.bfloat16)] * CHUNKS,
        compiler_params=pltpu.CompilerParams(
            collective_id=0, has_side_effects=True, vmem_limit_bytes=60 * 1024 * 1024
        ),
    )(amplitudes, integrals, ab_slot, cd_pick, jnp.transpose(wanted, (0, 2, 1)), kept_count)


def solution(mesh):
    in_specs = (
        P("pair", "col"),
        P("col", "pair", None, None),
        P("col", "pair"),
        P("col", "pair"),
        P(),
        P(),
    )
    out_specs = P("pair", "col")
    run = functools.partial(body, mesh.shape["pair"], mesh.shape["col"])
    return jax.shard_map(run, mesh=mesh, in_specs=in_specs, out_specs=out_specs, check_vma=False)
```

```python
import functools

import jax
import jax.numpy as jnp
from jax import lax
from jax.experimental import pallas as pl
from jax.experimental.pallas import tpu as pltpu
from jax.sharding import PartitionSpec as P

TILE = 128
ABT_DEV = 16
CAP = 2
PIECES = (32, 32, 32, 32)
CHUNKS = len(PIECES)
STARTS = tuple(sum(PIECES[:i]) for i in range(CHUNKS))
MESH = pl.DeviceIdType.MESH


def kernel(
    n_pair, n_col, slots,
    amp_ref, int_ref, ab_in, pick_in, wanted_in, count_in,
    out_ref,
    ab_ref, pick_ref, wanted_ref, count_ref, list_sem,
    tiles, pack, lhs, parts, table_v, table_s, wide, total_v,
    tile_sem, own_sem, table_sem, t_send, t_recv, v_send, v_recv, a_send, a_recv, *vall,
):
    pair = lax.axis_index("pair")
    col = lax.axis_index("col")
    n_tiles = n_col * CAP
    depth = CAP * TILE
    places = ABT_DEV * n_tiles
    lot_size = wide.shape[2] // TILE
    n_lots = n_tiles // lot_size

    barrier = pltpu.get_barrier_semaphore()

    root = n_col - 1
    last = col == root

    def greet_pair(step, carry):
        peer = lax.rem(pair + step, n_pair)
        pl.semaphore_signal(barrier, inc=1, device_id=(peer, col), device_id_type=MESH)
        return carry

    lax.fori_loop(1, n_pair, greet_pair, 0)

    lists = [
        pltpu.make_async_copy(source, target, list_sem.at[index])
        for index, (source, target) in enumerate(
            ((ab_in, ab_ref), (pick_in, pick_ref), (count_in, count_ref), (wanted_in, wanted_ref))
        )
    ]
    for copy in lists:
        copy.start()

    def v_copy(step, chunk, source):
        peer = lax.rem(pair + step, n_pair)
        return pltpu.make_async_remote_copy(
            src_ref=int_ref.at[0, :, pl.ds(STARTS[chunk], PIECES[chunk]), :],
            dst_ref=vall[chunk].at[pl.ds(source * slots, slots)],
            send_sem=v_send.at[step, chunk],
            recv_sem=v_recv.at[step, chunk],
            device_id=(peer, col),
            device_id_type=MESH,
        )

    def tile_copy(tile):
        return pltpu.make_async_copy(
            amp_ref.at[:, pl.ds(pl.multiple_of(tile * TILE, TILE), TILE)], tiles.at[tile], tile_sem.at[tile]
        )

    n_held = tiles.shape[0]
    for tile in range(n_held):
        tile_copy(tile).start()

    def own_copy(chunk):
        return pltpu.make_async_copy(
            int_ref.at[0, :, pl.ds(STARTS[chunk], PIECES[chunk]), :],
            vall[chunk].at[pl.ds(pair * slots, slots)],
            own_sem.at[chunk],
        )

    for chunk in range(CHUNKS):
        own_copy(chunk).start()

    @pl.when(jnp.logical_not(last))
    def _():
        pl.semaphore_wait(barrier, n_pair - 1)
        pl.semaphore_signal(barrier, inc=1, device_id=(pair, root), device_id_type=MESH)

    @pl.when(last)
    def _():
        pl.semaphore_wait(barrier, n_pair - 1 + n_col - 1)

    for step in range(1, n_pair):
        v_copy(step, 0, pair).start()

    @pl.when(last)
    def _():
        def release(peer, carry):
            pl.semaphore_signal(barrier, inc=1, device_id=(pair, peer), device_id_type=MESH)
            return carry

        lax.fori_loop(0, n_col - 1, release, 0)

    for copy in lists:
        copy.wait()
    lane = lax.broadcasted_iota(jnp.int32, (slots, slots), 1)
    row = lax.broadcasted_iota(jnp.int32, (slots, slots), 0)
    key_row = ab_ref[...] * n_tiles + pick_ref[...]
    key = jnp.sum(jnp.where(lane == row, key_row, 0), axis=1, keepdims=True)
    number = pair * slots + lax.broadcasted_iota(jnp.int32, (slots, 1), 0)
    key = jnp.where(number < count_ref[col], key, -1)
    place = lax.broadcasted_iota(jnp.int32, (slots, places), 1)
    parts[pair] = jnp.sum(jnp.where(place == key, number + 1, 0), axis=0, keepdims=True)
    for chunk in range(CHUNKS):
        vall[chunk][n_pair * slots] = jnp.zeros((PIECES[chunk], TILE), jnp.bfloat16)

    def t_copy(step, source):
        peer = lax.rem(pair + step, n_pair)
        return pltpu.make_async_remote_copy(
            src_ref=parts.at[source],
            dst_ref=parts.at[source],
            send_sem=t_send.at[step],
            recv_sem=t_recv.at[step],
            device_id=(peer, col),
            device_id_type=MESH,
        )

    def a_copy(step, source):
        peer = lax.rem(col + step, n_col)
        return pltpu.make_async_remote_copy(
            src_ref=pack.at[step],
            dst_ref=lhs.at[:, pl.ds(pl.multiple_of(source * depth, depth), depth)],
            send_sem=a_send.at[step],
            recv_sem=a_recv.at[step],
            device_id=(pair, peer),
            device_id_type=MESH,
        )

    for step in range(1, n_pair):
        t_copy(step, pair).start()
    for chunk in range(1, CHUNKS):
        for step in range(1, n_pair):
            v_copy(step, chunk, pair).start()

    def requested(owner, k):
        return tiles[wanted_ref[owner, k, col]]

    for tile in range(n_held):
        tile_copy(tile).wait()

    @pl.when(jnp.logical_not(last))
    def _():
        pl.semaphore_wait(barrier, 1)

    def send(step, carry):
        owner = lax.rem(col + step, n_col)
        for k in range(CAP):
            pack[step, :, k * TILE : (k + 1) * TILE] = requested(owner, k)
        a_copy(step, col).start()
        return carry

    lax.fori_loop(1, n_col, send, 0)
    for k in range(CAP):
        lhs[:, pl.ds(pl.multiple_of(col * depth + k * TILE, TILE), TILE)] = requested(col, k)

    for step in range(1, n_pair):
        t_copy(step, lax.rem(pair + n_pair - step, n_pair)).wait_recv()
    found = parts[0]
    for index in range(1, n_pair):
        found = found + parts[index]
    table_v[...] = jnp.where(found == 0, n_pair * slots, found - 1)
    to_scalar = pltpu.make_async_copy(table_v, table_s, table_sem)
    to_scalar.start()
    to_scalar.wait()
    for chunk in range(CHUNKS):
        own_copy(chunk).wait()

    def arrived(step, carry):
        a_copy(step, lax.rem(col + n_col - step, n_col)).wait_recv()
        return carry

    lax.fori_loop(1, n_col, arrived, 0)
    for chunk in range(CHUNKS):
        for step in range(1, n_pair):
            v_copy(step, chunk, lax.rem(pair + n_pair - step, n_pair)).wait_recv()
        piece = PIECES[chunk]
        group = 2 * TILE // piece
        for block in range(ABT_DEV // group):
            part = block % 2

            def lot_dot(lot):
                for inner in range(group):
                    first = (block * group + inner) * n_tiles + lot * lot_size
                    for tile in range(lot_size):
                        wide[part, inner * piece : (inner + 1) * piece, tile * TILE : (tile + 1) * TILE] = vall[chunk][
                            table_s[0, first + tile]
                        ]
                columns = lhs[...] if n_lots == 1 else lhs[:, pl.ds(pl.multiple_of(lot * wide.shape[2], TILE), wide.shape[2])]
                return lax.dot_general(columns, wide[part], (((1,), (1,)), ((), ())), preferred_element_type=jnp.float32)

            def add_lot(lot, carry):
                total_v[...] += lot_dot(lot)
                return carry

            if n_lots == 1:
                total = lot_dot(0)
            else:
                total_v[...] = jnp.zeros_like(total_v)
                lax.fori_loop(0, n_lots, add_lot, 0)
                total = total_v[...]
            total = total.astype(jnp.bfloat16)
            for inner in range(group):
                first = (block * group + inner) * TILE + STARTS[chunk]
                out_ref[:, first : first + piece] = total[:, inner * piece : (inner + 1) * piece]

    def sent(step, carry):
        a_copy(step, col).wait_send()
        return carry

    lax.fori_loop(1, n_col, sent, 0)
    for step in range(1, n_pair):
        t_copy(step, pair).wait_send()
        for chunk in range(CHUNKS):
            v_copy(step, chunk, pair).wait_send()


def body(n_pair, n_col, amplitudes, integrals, ab_slot, cd_pick, wanted, kept_count):
    pairs = amplitudes.shape[0]
    slots = integrals.shape[1]
    n_held = amplitudes.shape[1] // TILE
    depth = CAP * TILE
    places = ABT_DEV * n_col * CAP
    lot_depth = min(16, n_col) * depth
    vmem = pl.BlockSpec(memory_space=pltpu.VMEM)
    anywhere = pl.BlockSpec(memory_space=pl.ANY)
    dma = pltpu.SemaphoreType.DMA
    return pl.pallas_call(
        functools.partial(kernel, n_pair, n_col, slots),
        out_shape=pltpu.VMEM((pairs, ABT_DEV * TILE), jnp.bfloat16),
        in_specs=[anywhere] * 6,
        out_specs=vmem,
        scratch_shapes=[
            pltpu.VMEM(ab_slot.shape, jnp.int32),
            pltpu.VMEM(cd_pick.shape, jnp.int32),
            pltpu.SMEM((n_col, CAP, n_col), jnp.int32),
            pltpu.SMEM(kept_count.shape, jnp.int32),
            dma((4,)),
            pltpu.VMEM((n_held, pairs, TILE), jnp.bfloat16),
            pltpu.VMEM((n_col, pairs, depth), jnp.bfloat16),
            pltpu.VMEM((pairs, n_col * depth), jnp.bfloat16),
            pltpu.VMEM((n_pair, 1, places), jnp.int32),
            pltpu.VMEM((1, places), jnp.int32),
            pltpu.SMEM((1, places), jnp.int32),
            pltpu.VMEM((2, 2 * TILE, lot_depth), jnp.bfloat16),
            pltpu.VMEM((pairs, 2 * TILE), jnp.float32),
            dma((n_held,)), dma((CHUNKS,)), dma,
            dma((n_pair,)), dma((n_pair,)),
            dma((n_pair, CHUNKS)), dma((n_pair, CHUNKS)),
            dma((n_col,)), dma((n_col,)),
        ]
        + [pltpu.VMEM((n_pair * slots + 1, piece, TILE), jnp.bfloat16) for piece in PIECES],
        compiler_params=pltpu.CompilerParams(
            collective_id=0, has_side_effects=True, vmem_limit_bytes=60 * 1024 * 1024
        ),
    )(amplitudes, integrals, ab_slot, cd_pick, jnp.transpose(wanted, (0, 2, 1)), kept_count)


def solution(mesh):
    in_specs = (
        P("pair", "col"),
        P("col", "pair", None, None),
        P("col", "pair"),
        P("col", "pair"),
        P(),
        P(),
    )
    out_specs = P("pair", "col")
    run = functools.partial(body, mesh.shape["pair"], mesh.shape["col"])
    return jax.shard_map(run, mesh=mesh, in_specs=in_specs, out_specs=out_specs, check_vma=False)
```

```python
import functools

import jax
import jax.numpy as jnp
from jax import lax
from jax.experimental import pallas as pl
from jax.experimental.pallas import tpu as pltpu
from jax.sharding import PartitionSpec as P

TILE = 128
ABT_DEV = 16
CAP = 2
PIECES = (32, 32, 32, 32)
CHUNKS = len(PIECES)
STARTS = tuple(sum(PIECES[:i]) for i in range(CHUNKS))
MESH = pl.DeviceIdType.MESH


def kernel(
    n_pair, n_col, slots,
    amp_ref, int_ref, ab_in, pick_in, wanted_in, count_in,
    out_ref,
    ab_ref, pick_ref, wanted_ref, count_ref, list_sem,
    tiles, pack, lhs, parts, table_v, table_s, wide, total_v,
    tile_sem, own_sem, table_sem, t_send, t_recv, v_send, v_recv, a_send, a_recv, *vall,
):
    pair = lax.axis_index("pair")
    col = lax.axis_index("col")
    n_tiles = n_col * CAP
    depth = CAP * TILE
    places = ABT_DEV * n_tiles
    lot_size = wide.shape[2] // TILE
    n_lots = n_tiles // lot_size

    barrier = pltpu.get_barrier_semaphore()

    root = n_col - 1
    last = col == root

    def greet_pair(step, carry):
        peer = lax.rem(pair + step, n_pair)
        pl.semaphore_signal(barrier, inc=1, device_id=(peer, col), device_id_type=MESH)
        return carry

    lax.fori_loop(1, n_pair, greet_pair, 0)

    def v_copy(step, chunk, source):
        peer = lax.rem(pair + step, n_pair)
        return pltpu.make_async_remote_copy(
            src_ref=int_ref.at[0, :, pl.ds(STARTS[chunk], PIECES[chunk]), :],
            dst_ref=vall[chunk].at[pl.ds(source * slots, slots)],
            send_sem=v_send.at[step, chunk],
            recv_sem=v_recv.at[step, chunk],
            device_id=(peer, col),
            device_id_type=MESH,
        )

    def tile_copy(tile):
        return pltpu.make_async_copy(
            amp_ref.at[:, pl.ds(pl.multiple_of(tile * TILE, TILE), TILE)], tiles.at[tile], tile_sem.at[tile]
        )

    n_held = tiles.shape[0]
    def own_copy(chunk):
        return pltpu.make_async_copy(
            int_ref.at[0, :, pl.ds(STARTS[chunk], PIECES[chunk]), :],
            vall[chunk].at[pl.ds(pair * slots, slots)],
            own_sem.at[chunk],
        )

    @pl.when(jnp.logical_not(last))
    def _():
        pl.semaphore_wait(barrier, n_pair - 1)
        pl.semaphore_signal(barrier, inc=1, device_id=(pair, root), device_id_type=MESH)

    @pl.when(last)
    def _():
        pl.semaphore_wait(barrier, n_pair - 1 + n_col - 1)

    for step in range(1, n_pair):
        v_copy(step, 0, pair).start()

    @pl.when(last)
    def _():
        def release(peer, carry):
            pl.semaphore_signal(barrier, inc=1, device_id=(pair, peer), device_id_type=MESH)
            return carry

        lax.fori_loop(0, n_col - 1, release, 0)

    lists = [
        pltpu.make_async_copy(source, target, list_sem.at[index])
        for index, (source, target) in enumerate(
            ((ab_in, ab_ref), (pick_in, pick_ref), (count_in, count_ref), (wanted_in, wanted_ref))
        )
    ]
    for copy in lists:
        copy.start()

    for tile in range(n_held):
        tile_copy(tile).start()

    for chunk in range(CHUNKS):
        own_copy(chunk).start()

    for copy in lists:
        copy.wait()
    lane = lax.broadcasted_iota(jnp.int32, (slots, slots), 1)
    row = lax.broadcasted_iota(jnp.int32, (slots, slots), 0)
    key_row = ab_ref[...] * n_tiles + pick_ref[...]
    key = jnp.sum(jnp.where(lane == row, key_row, 0), axis=1, keepdims=True)
    number = pair * slots + lax.broadcasted_iota(jnp.int32, (slots, 1), 0)
    key = jnp.where(number < count_ref[col], key, -1)
    place = lax.broadcasted_iota(jnp.int32, (slots, places), 1)
    parts[pair] = jnp.sum(jnp.where(place == key, number + 1, 0), axis=0, keepdims=True)
    for chunk in range(CHUNKS):
        vall[chunk][n_pair * slots] = jnp.zeros((PIECES[chunk], TILE), jnp.bfloat16)

    def t_copy(step, source):
        peer = lax.rem(pair + step, n_pair)
        return pltpu.make_async_remote_copy(
            src_ref=parts.at[source],
            dst_ref=parts.at[source],
            send_sem=t_send.at[step],
            recv_sem=t_recv.at[step],
            device_id=(peer, col),
            device_id_type=MESH,
        )

    def a_copy(step, source):
        peer = lax.rem(col + step, n_col)
        return pltpu.make_async_remote_copy(
            src_ref=pack.at[step],
            dst_ref=lhs.at[:, pl.ds(pl.multiple_of(source * depth, depth), depth)],
            send_sem=a_send.at[step],
            recv_sem=a_recv.at[step],
            device_id=(pair, peer),
            device_id_type=MESH,
        )

    for step in range(1, n_pair):
        t_copy(step, pair).start()
    for chunk in range(1, CHUNKS):
        for step in range(1, n_pair):
            v_copy(step, chunk, pair).start()

    def requested(owner, k):
        return tiles[wanted_ref[owner, k, col]]

    for tile in range(n_held):
        tile_copy(tile).wait()

    @pl.when(jnp.logical_not(last))
    def _():
        pl.semaphore_wait(barrier, 1)

    def send(step, carry):
        owner = lax.rem(col + step, n_col)
        for k in range(CAP):
            pack[step, :, k * TILE : (k + 1) * TILE] = requested(owner, k)
        a_copy(step, col).start()
        return carry

    lax.fori_loop(1, n_col, send, 0)
    for k in range(CAP):
        lhs[:, pl.ds(pl.multiple_of(col * depth + k * TILE, TILE), TILE)] = requested(col, k)

    for step in range(1, n_pair):
        t_copy(step, lax.rem(pair + n_pair - step, n_pair)).wait_recv()
    found = parts[0]
    for index in range(1, n_pair):
        found = found + parts[index]
    table_v[...] = jnp.where(found == 0, n_pair * slots, found - 1)
    to_scalar = pltpu.make_async_copy(table_v, table_s, table_sem)
    to_scalar.start()
    to_scalar.wait()
    for chunk in range(CHUNKS):
        own_copy(chunk).wait()

    def sent(step, carry):
        a_copy(step, col).wait_send()
        return carry

    def arrived(step, carry):
        a_copy(step, lax.rem(col + n_col - step, n_col)).wait_recv()
        return carry

    lax.fori_loop(1, n_col, arrived, 0)
    for chunk in range(CHUNKS):
        if chunk == CHUNKS - 1:
            lax.fori_loop(1, n_col, sent, 0)
            for step in range(1, n_pair):
                t_copy(step, pair).wait_send()
                for before in range(chunk):
                    v_copy(step, before, pair).wait_send()
        for step in range(1, n_pair):
            v_copy(step, chunk, lax.rem(pair + n_pair - step, n_pair)).wait_recv()
        piece = PIECES[chunk]
        group = 2 * TILE // piece
        for block in range(ABT_DEV // group):
            part = block % 2

            def lot_dot(lot):
                for inner in range(group):
                    first = (block * group + inner) * n_tiles + lot * lot_size
                    for tile in range(lot_size):
                        wide[part, inner * piece : (inner + 1) * piece, tile * TILE : (tile + 1) * TILE] = vall[chunk][
                            table_s[0, first + tile]
                        ]
                columns = lhs[...] if n_lots == 1 else lhs[:, pl.ds(pl.multiple_of(lot * wide.shape[2], TILE), wide.shape[2])]
                return lax.dot_general(columns, wide[part], (((1,), (1,)), ((), ())), preferred_element_type=jnp.float32)

            def add_lot(lot, carry):
                total_v[...] += lot_dot(lot)
                return carry

            if n_lots == 1:
                total = lot_dot(0)
            else:
                total_v[...] = jnp.zeros_like(total_v)
                lax.fori_loop(0, n_lots, add_lot, 0)
                total = total_v[...]
            total = total.astype(jnp.bfloat16)
            for inner in range(group):
                first = (block * group + inner) * TILE + STARTS[chunk]
                out_ref[:, first : first + piece] = total[:, inner * piece : (inner + 1) * piece]
    for step in range(1, n_pair):
        v_copy(step, CHUNKS - 1, pair).wait_send()


def body(n_pair, n_col, amplitudes, integrals, ab_slot, cd_pick, wanted, kept_count):
    pairs = amplitudes.shape[0]
    slots = integrals.shape[1]
    n_held = amplitudes.shape[1] // TILE
    depth = CAP * TILE
    places = ABT_DEV * n_col * CAP
    lot_depth = min(16, n_col) * depth
    vmem = pl.BlockSpec(memory_space=pltpu.VMEM)
    anywhere = pl.BlockSpec(memory_space=pl.ANY)
    dma = pltpu.SemaphoreType.DMA
    return pl.pallas_call(
        functools.partial(kernel, n_pair, n_col, slots),
        out_shape=pltpu.VMEM((pairs, ABT_DEV * TILE), jnp.bfloat16),
        in_specs=[anywhere] * 6,
        out_specs=vmem,
        scratch_shapes=[
            pltpu.VMEM(ab_slot.shape, jnp.int32),
            pltpu.VMEM(cd_pick.shape, jnp.int32),
            pltpu.SMEM((n_col, CAP, n_col), jnp.int32),
            pltpu.SMEM(kept_count.shape, jnp.int32),
            dma((4,)),
            pltpu.VMEM((n_held, pairs, TILE), jnp.bfloat16),
            pltpu.VMEM((n_col, pairs, depth), jnp.bfloat16),
            pltpu.VMEM((pairs, n_col * depth), jnp.bfloat16),
            pltpu.VMEM((n_pair, 1, places), jnp.int32),
            pltpu.VMEM((1, places), jnp.int32),
            pltpu.SMEM((1, places), jnp.int32),
            pltpu.VMEM((2, 2 * TILE, lot_depth), jnp.bfloat16),
            pltpu.VMEM((pairs, 2 * TILE), jnp.float32),
            dma((n_held,)), dma((CHUNKS,)), dma,
            dma((n_pair,)), dma((n_pair,)),
            dma((n_pair, CHUNKS)), dma((n_pair, CHUNKS)),
            dma((n_col,)), dma((n_col,)),
        ]
        + [pltpu.VMEM((n_pair * slots + 1, piece, TILE), jnp.bfloat16) for piece in PIECES],
        compiler_params=pltpu.CompilerParams(
            collective_id=0, has_side_effects=True, vmem_limit_bytes=60 * 1024 * 1024
        ),
    )(amplitudes, integrals, ab_slot, cd_pick, jnp.transpose(wanted, (0, 2, 1)), kept_count)


def solution(mesh):
    in_specs = (
        P("pair", "col"),
        P("col", "pair", None, None),
        P("col", "pair"),
        P("col", "pair"),
        P(),
        P(),
    )
    out_specs = P("pair", "col")
    run = functools.partial(body, mesh.shape["pair"], mesh.shape["col"])
    return jax.shard_map(run, mesh=mesh, in_specs=in_specs, out_specs=out_specs, check_vma=False)
```
